32 devices in a mesh: gx: 8 (over z, y), gy: 4 (over x, core).
Axes of the slice: x: 2, y: 2, z: 4, core: 2. Of those that a mesh axis runs over, the one named last changes fastest.
Arguments:
- fuel: float32 [16, 768, 384], P('gx', 'gy'), may hold values from -41 to 41, as said below
- oxidizer: float32 [16, 768, 384], P('gx', 'gy'), may hold values from -41 to 41, as said below
- kappa: float32 [16, 768, 384], P('gx', 'gy'), may hold values from 0.05 to 0.5
- rate: float32 [16, 768, 384], P('gx', 'gy'), may hold values from 0.5 to 5
Outputs:
- fuel_next: float32 [16, 768, 384], P('gx', 'gy')
- oxid_next: float32 [16, 768, 384], P('gx', 'gy')
- r_factor: float32 [384, 384], replicated
The draws below stay inside these ranges and needn't reach their ends.
Inputs may be any that keep to these rules, and one draw needn't show every extreme that they name: `fuel`: A real-valued field. `oxidizer`: A real-valued field.
All inputs are finite; a program needn't handle non-finite values.
Results may differ from the reference program's by a relative error of at most 0.000067.
Values sent between devices are 32-bit elements; how exact they have to be, the bound alone decides.
A program may use at most 64 MiB of HBM per device.

```python
import math
import jax
import jax.numpy as jnp
from jax import lax

NZ = 384
NX = 16
NY = 768


def field_draw(key, salt):
    key = jax.random.fold_in(key, salt)
    keys = jax.random.split(key, 5)
    ramp = jnp.arange(NX, dtype=jnp.float32) / max(NX - 1, 1)
    row_scale = jnp.exp(jax.random.uniform(keys[0], (NX, NY), jnp.float32, math.log(0.5), math.log(1.5)))
    row_scale = row_scale * (0.5 + ramp)[:, None]
    col_scale = jnp.exp(jax.random.uniform(keys[1], (NZ,), jnp.float32, math.log(0.3), math.log(3.0)))
    profile = jax.random.uniform(keys[2], (NZ,), jnp.float32, -1.0, 1.0)
    noise = jnp.clip(jax.random.normal(keys[3], (NX, NY, NZ), jnp.float32), -3.0, 3.0)
    common = jnp.clip(jax.random.normal(keys[4], (NX, NY), jnp.float32), -3.0, 3.0)
    inner = noise + common[:, :, None] * profile[None, None, :]
    return (row_scale[:, :, None] * col_scale[None, None, :] * inner).astype(jnp.float32)


def draw_fuel(key, part):
    return field_draw(key, 11)


def draw_oxidizer(key, part):
    return field_draw(key, 23)


def levels(stream_key, extent, shards, smallest, largest):
    factor_of, own = 1.0, jax.random.fold_in(stream_key, 6)
    for position, parts in shards:
        steps = jnp.exp(jax.random.uniform(jax.random.fold_in(own, position), (parts,), jnp.float32, smallest / len(shards), largest / len(shards)))
        factor_of = factor_of * jnp.repeat(steps, extent[position] // parts).reshape([-1 if axis == position else 1 for axis in range(len(extent))])
    return factor_of


def setup_inputs(seed: int = 0) -> dict:
    key_of = jax.random.split(jax.random.key(seed), 5)
    fuel = draw_fuel(jax.random.fold_in(key_of[4], 71), 0)
    oxidizer = draw_oxidizer(jax.random.fold_in(key_of[4], 71), 0)
    kappa = jnp.clip(0.05 + 0.45 * jax.random.uniform(key_of[2], (NX, NY, NZ), jnp.float32) ** levels(key_of[2], (NX, NY, NZ), ((0, 8), (1, 4)), -0.2, 0.2), 0.05, 0.5)
    rate = jnp.clip(jnp.exp(math.log(5.0) - 2.3025851 * jax.random.uniform(key_of[3], (NX, NY, NZ), jnp.float32) ** levels(key_of[3], (NX, NY, NZ), ((0, 8), (1, 4)), -0.2, 0.2)), 0.5, 5.0)
    return {"fuel": fuel, "oxidizer": oxidizer, "kappa": kappa, "rate": rate}


def diffuse(field, kappa):
    padded = jnp.pad(field, 1)
    kpad = jnp.pad(kappa, 1)
    total = jnp.zeros_like(field)
    center = padded[1:-1, 1:-1, 1:-1]
    kcenter = kpad[1:-1, 1:-1, 1:-1]
    for axis in range(3):
        for offset in (0, 2):
            index = [slice(1, -1)] * 3
            index[axis] = slice(offset, offset + field.shape[axis])
            index = tuple(index)
            total = total + 0.5 * (kcenter + kpad[index]) * (padded[index] - center)
    return total

def reference(fuel, oxidizer, kappa, rate):
    prod = fuel * oxidizer
    react = rate * prod / jnp.sqrt(1.0 + prod * prod)
    fuel_next = fuel + 0.15 * (diffuse(fuel, kappa) - react)
    oxid_next = oxidizer + 0.15 * (diffuse(oxidizer, kappa) + react)
    rows = 2 * fuel.shape[0] * fuel.shape[1]
    flat_a = fuel_next.reshape(-1, fuel.shape[2])
    flat_b = oxid_next.reshape(-1, fuel.shape[2])
    dims = (((0,), (0,)), ((), ()))
    gram = lax.dot_general(flat_a, flat_a, dims, precision=lax.Precision.HIGHEST)
    gram = gram + lax.dot_general(flat_b, flat_b, dims, precision=lax.Precision.HIGHEST)
    gram = gram / rows
    lower = jnp.linalg.cholesky(gram)
    return (fuel_next, oxid_next, lower.T)
```

```python
import functools

import jax
import jax.numpy as jnp
from jax import lax
from jax.experimental import pallas as pl
from jax.experimental.pallas import tpu as pltpu
from jax.sharding import PartitionSpec as P

MESH = pl.DeviceIdType.MESH
TILE = 8
LANES = 128
HIGHEST = lax.Precision.HIGHEST
GROUP = 4
AHEAD = 3


def peer(index, stage, k):
    axis, stride, size = stage
    mine = lax.rem(index[axis] // stride, size)
    other = lax.rem(mine + k, size)
    place = dict(index)
    place[axis] = index[axis] + (other - mine) * stride
    return mine, other, (place["gx"], place["gy"])


def sum_over_all(index, stages, source, out_ref, inbox, held, sems):
    count = len(stages)
    length = source.shape[0]
    starts = []
    start = 0
    for s, stage in enumerate(stages):
        size = stage[2]
        length //= size
        sent = []
        for k in range(1, size):
            mine, other, device = peer(index, stage, k)
            sent.append(
                pltpu.make_async_remote_copy(
                    src_ref=source.at[pl.ds(pl.multiple_of(other * length, TILE), length)],
                    dst_ref=inbox[s].at[k - 1],
                    send_sem=sems[0].at[s, k - 1],
                    recv_sem=sems[1].at[s, k - 1],
                    device_id=device,
                    device_id_type=MESH,
                )
            )
            sent[-1].start()
        for copy in sent:
            copy.wait_recv()
        total = source[pl.ds(pl.multiple_of(mine * length, TILE), length)]
        for k in range(1, size):
            total = total + inbox[s][k - 1]
        held[s][...] = total
        for copy in sent:
            copy.wait_send()
        source = held[s]
        start = start + mine * length
        starts.append((start, length))
    part = pl.ds(pl.multiple_of(start, TILE), length)
    out_ref[part] = source[...]
    for s in reversed(range(count)):
        start, length = starts[s]
        part = pl.ds(pl.multiple_of(start, TILE), length)
        sent = []
        for k in range(1, stages[s][2]):
            sent.append(
                pltpu.make_async_remote_copy(
                    src_ref=out_ref.at[part],
                    dst_ref=out_ref.at[part],
                    send_sem=sems[2].at[s, k - 1],
                    recv_sem=sems[3].at[s, k - 1],
                    device_id=peer(index, stages[s], k)[2],
                    device_id_type=MESH,
                )
            )
            sent[-1].start()
        for copy in sent:
            copy.wait()


def update_kernel(
    n, m, rows, parts, stages,
    f_hbm, o_hbm, k_hbm, r_hbm, fn_hbm, on_hbm, g_out,
    f_ref, o_ref, k_ref, r_ref, fn_ref, on_ref, xlo, xhi, ylo, yhi, gram, passing,
    local_sem, xs_sem, xr_sem, ys_sem, yr_sem, ps_sem, pr_sem, *scratch
):
    i, j = lax.axis_index("gx"), lax.axis_index("gy")
    index = {"gx": i, "gy": j}
    planes, width, depth = f_ref.shape
    step = width // parts
    sides = (
        (i < n - 1, i > 0, i + 1, j),
        (i > 0, i < n - 1, i - 1, j),
        (j < m - 1, j > 0, i, j + 1),
        (j > 0, j < m - 1, i, j - 1),
    )
    z, odd, depth_z = i // 2, lax.rem(i, 2) == 1, n // 2
    rising = lambda pair: (pair + 1) * parts // depth_z
    falling = lambda pair: (depth_z - 1 - pair) * parts // depth_z
    if n % 2 or n < 4:
        indirect = (0, 0)
        relayed = 0
    else:
        indirect = (jnp.where(odd, falling(z), 0), jnp.where(odd, 0, rising(z - 1)))
        relayed = jnp.where(odd, rising(z - 1), falling(z))
    via = (i - 1, i + 1)
    onward = jnp.where(odd, i - 2, i + 2)
    lands = (jnp.logical_not(odd), odd)
    relayed = jnp.where(odd, jnp.where(z > 0, relayed, 0), jnp.where(z < depth_z - 1, relayed, 0))
    greets = sides + ((i < n - 2, None, i + 2, j), (i > 1, None, i - 2, j))
    barrier = pltpu.get_barrier_semaphore()
    greeted = sum(has.astype(jnp.int32) for has, _, _, _ in greets)
    for has, _, a, b in greets:
        @pl.when(has)
        def _(a=a, b=b):
            pl.semaphore_signal(barrier, inc=1, device_id=(a, b), device_id_type=MESH)
    for stage in stages:
        for k in range(1, stage[2]):
            pl.semaphore_signal(barrier, inc=1, device_id=peer(index, stage, k)[2], device_id_type=MESH)
            greeted = greeted + 1
    pl.semaphore_wait(barrier, greeted)
    fields = (f_hbm, o_hbm, k_hbm)

    def x_copies(side, part):
        _, _, a, b = sides[side]
        cut = pl.ds(part * step, step)
        return [
            pltpu.make_async_remote_copy(
                src_ref=ref.at[(planes - 1, 0)[side], cut],
                dst_ref=(xlo, xhi)[side].at[t, cut],
                send_sem=xs_sem.at[side, part, t],
                recv_sem=xr_sem.at[side, part, t],
                device_id=(a, b),
                device_id_type=MESH,
            )
            for t, ref in enumerate(fields)
        ]

    def to_relay(side, part):
        cut = pl.ds(part * step, step)
        return [
            pltpu.make_async_remote_copy(
                src_ref=ref.at[(planes - 1, 0)[side], cut],
                dst_ref=passing.at[t, cut],
                send_sem=xs_sem.at[side, part, t],
                recv_sem=pr_sem.at[part, t],
                device_id=(via[side], j),
                device_id_type=MESH,
            )
            for t, ref in enumerate(fields)
        ]

    def from_relay(side, part):
        cut = pl.ds(part * step, step)
        return [
            pltpu.make_async_remote_copy(
                src_ref=passing.at[t, cut],
                dst_ref=(xlo, xhi)[side].at[t, cut],
                send_sem=ps_sem.at[part, t],
                recv_sem=xr_sem.at[side, part, t],
                device_id=(onward, j),
                device_id_type=MESH,
            )
            for t in range(3)
        ]

    def y_copies(side):
        _, _, a, b = sides[2 + side]
        return [
            pltpu.make_async_remote_copy(
                src_ref=ref.at[:, pl.ds((width - TILE, 0)[side], TILE)],
                dst_ref=(ylo, yhi)[side].at[t],
                send_sem=ys_sem.at[side, t],
                recv_sem=yr_sem.at[side, t],
                device_id=(a, b),
                device_id_type=MESH,
            )
            for t, ref in enumerate(fields)
        ]

    for side in range(2):
        @pl.when(sides[2 + side][0])
        def _(side=side):
            for copy in y_copies(side):
                copy.start()
    for part in range(parts):
        for side in range(2):
            @pl.when(sides[side][0] & (part >= indirect[side]))
            def _(side=side, part=part):
                for copy in x_copies(side, part):
                    copy.start()

            @pl.when(sides[side][0] & (part < indirect[side]))
            def _(side=side, part=part):
                for copy in to_relay(side, part):
                    copy.start()
    loads = [
        pltpu.make_async_copy(src, dst, local_sem.at[t])
        for t, (src, dst) in enumerate(((f_hbm, f_ref), (o_hbm, o_ref), (k_hbm, k_ref), (r_hbm, r_ref)))
    ]
    for copy in loads:
        copy.start()
    for copy in loads:
        copy.wait()
    for side in range(2):
        @pl.when(sides[2 + side][1])
        def _(side=side):
            for copy in y_copies(side):
                copy.wait_recv()

    row = lax.broadcasted_iota(jnp.int32, (step, depth), 0)
    lane = lax.broadcasted_iota(jnp.int32, (step, depth), 1)
    refs = (f_ref, o_ref, k_ref)
    zero = jnp.zeros((step, depth), jnp.float32)
    zrow = jnp.zeros((1, depth), jnp.float32)
    dims = (((0,), (0,)), ((), ()))
    for q in range(parts):
        @pl.when(q < relayed)
        def _(q=q):
            for copy in to_relay(0, q):
                copy.wait_recv()

        for side in range(2):
            @pl.when((q < relayed) & lands[side])
            def _(side=side, q=q):
                for copy in from_relay(side, q):
                    copy.start()

        for side in range(2):
            @pl.when(sides[side][1])
            def _(side=side, q=q):
                for copy in x_copies(side, q):
                    copy.wait_recv()
        y = q * step
        part = pl.ds(y, step)
        for x in range(planes):
            center = [ref[x, part] for ref in refs]
            sets = []
            if x == 0:
                sets.append([jnp.where(i > 0, xlo[t, part], zero) for t in range(3)])
            else:
                sets.append([ref[x - 1, part] for ref in refs])
            if x == planes - 1:
                sets.append([jnp.where(i < n - 1, xhi[t, part], zero) for t in range(3)])
            else:
                sets.append([ref[x + 1, part] for ref in refs])
            if y == 0:
                before = [jnp.where(j > 0, ylo[t, x, TILE - 1:TILE], zrow) for t in range(3)]
            else:
                before = [ref[x, y - 1:y] for ref in refs]
            if y + step == width:
                after = [jnp.where(j < m - 1, yhi[t, x, 0:1], zrow) for t in range(3)]
            else:
                after = [ref[x, y + step:y + step + 1] for ref in refs]
            sets.append([jnp.where(row == 0, b, pltpu.roll(c, 1, 0)) for b, c in zip(before, center)])
            sets.append([jnp.where(row == step - 1, a, pltpu.roll(c, step - 1, 0)) for a, c in zip(after, center)])
            sets.append([jnp.where(lane == 0, 0.0, pltpu.roll(c, 1, 1)) for c in center])
            sets.append([jnp.where(lane == depth - 1, 0.0, pltpu.roll(c, depth - 1, 1)) for c in center])
            fc, oc, kc = center
            df, do = zero, zero
            for fs, os, ks in sets:
                weight = 0.5 * (kc + ks)
                df = df + weight * (fs - fc)
                do = do + weight * (os - oc)
            prod = fc * oc
            react = r_ref[x, part] * prod / jnp.sqrt(1.0 + prod * prod)
            fn_ref[x, part] = fc + 0.15 * (df - react)
            on_ref[x, part] = oc + 0.15 * (do + react)
        u = jnp.concatenate([ref[x, part] for ref in (fn_ref, on_ref) for x in range(planes)], axis=0)
        at = 0
        for a in range(0, depth, LANES):
            total = lax.dot_general(u[:, a:a + LANES], u[:, a:], dims, precision=HIGHEST, preferred_element_type=jnp.float32)
            for b in range(0, depth - a, LANES):
                block = total[:, b:b + LANES]
                held_rows = slice(at, at + LANES)
                gram[held_rows] = block if q == 0 else gram[held_rows] + block
                at += LANES
    stores = [
        pltpu.make_async_copy(src, dst, local_sem.at[t])
        for t, (src, dst) in enumerate(((fn_ref, fn_hbm), (on_ref, on_hbm)))
    ]
    for copy in stores:
        copy.start()
    gram[...] = gram[...] / rows
    if stages:
        count = len(stages)
        sum_over_all(index, stages, gram, g_out, scratch[:count], scratch[count:2 * count], scratch[2 * count:])
    else:
        g_out[...] = gram[...]
    for side in range(2):
        @pl.when(sides[2 + side][0])
        def _(side=side):
            for copy in y_copies(side):
                copy.wait_send()

        @pl.when(sides[side][0])
        def _(side=side):
            for part in range(parts):
                for copy in x_copies(side, part):
                    copy.wait_send()

    for part in range(parts):
        @pl.when(part < relayed)
        def _(part=part):
            for copy in from_relay(0, part):
                copy.wait_send()
    for copy in stores:
        copy.wait()


def update(n, m, rows, stages, fuel, oxidizer, kappa, rate):
    planes, width, depth = fuel.shape
    blocks = depth // LANES
    parts = 4 if width % (4 * TILE) == 0 else 1
    gram_rows = blocks * (blocks + 1) // 2 * LANES
    scratch = [pltpu.VMEM(fuel.shape, jnp.float32)] * 6
    scratch += [pltpu.VMEM((3, width, depth), jnp.float32)] * 2
    scratch += [pltpu.VMEM((3, planes, TILE, depth), jnp.float32)] * 2
    scratch += [pltpu.VMEM((gram_rows, LANES), jnp.float32)]
    scratch += [pltpu.VMEM((3, width, depth), jnp.float32)]
    scratch += [pltpu.SemaphoreType.DMA((4,))]
    scratch += [pltpu.SemaphoreType.DMA((2, parts, 3))] * 2
    scratch += [pltpu.SemaphoreType.DMA((2, 3))] * 2
    scratch += [pltpu.SemaphoreType.DMA((parts, 3))] * 2
    if stages:
        inbox, held, length = [], [], gram_rows
        for _, _, size in stages:
            length //= size
            inbox.append(pltpu.VMEM((size - 1, length, LANES), jnp.float32))
            held.append(pltpu.VMEM((length, LANES), jnp.float32))
        most = max(stage[2] for stage in stages)
        scratch += inbox + held + [pltpu.SemaphoreType.DMA((len(stages), most - 1))] * 4
    field = jax.ShapeDtypeStruct(fuel.shape, jnp.float32)
    any_spec = pl.BlockSpec(memory_space=pl.ANY)
    return pl.pallas_call(
        functools.partial(update_kernel, n, m, rows, parts, stages),
        out_shape=(field, field, jax.ShapeDtypeStruct((gram_rows, LANES), jnp.float32)),
        in_specs=[any_spec] * 4,
        out_specs=(any_spec, any_spec, pl.BlockSpec(memory_space=pltpu.VMEM)),
        scratch_shapes=scratch,
        compiler_params=pltpu.CompilerParams(collective_id=0, has_side_effects=True),
        name="update",
    )(fuel, oxidizer, kappa, rate)


def eliminate(a_ref, group, first, emit):
    width = a_ref.shape[1]
    tiles = range(width // LANES)
    sub = lax.broadcasted_iota(jnp.int32, (TILE, LANES), 0)
    lane = lax.broadcasted_iota(jnp.int32, (TILE, LANES), 1)
    before, upper = [], [[] for _ in tiles]
    for q in range(first, first + TILE * group, TILE):
        strips = [a_ref[q:q + TILE, t * LANES:(t + 1) * LANES] for t in tiles]
        for s, inv, low, rows in before:
            factors = []
            for k in range(TILE):
                value = column_of(strips[0], s + k)
                for j in range(k):
                    value = value - factors[j] * low[k, j]
                factors.append(value * inv[k])
            for t in tiles:
                for k in range(TILE):
                    strips[t] = strips[t] - factors[k] * rows[t][k]
        e = {}
        for k in range(TILE):
            column = column_of(strips[0], q + k)
            for i in range(k, TILE):
                e[i, k] = jnp.broadcast_to(column[i:i + 1], (TILE, LANES))
        inv, low = [], {}
        for k in range(TILE):
            inv.append(lax.rsqrt(e[k, k]))
            for i in range(k + 1, TILE):
                low[i, k] = e[i, k] * inv[k]
            for j in range(k + 1, TILE):
                for i in range(j, TILE):
                    e[i, j] = e[i, j] - low[i, k] * low[j, k]
        rows = []
        for t in tiles:
            made = []
            for k in range(TILE):
                value = jnp.broadcast_to(strips[t][k:k + 1], (TILE, LANES))
                for j in range(k):
                    value = value - low[k, j] * made[j]
                made.append(value * inv[k])
            rows.append(made)
            strip = made[0]
            for k in range(1, TILE):
                strip = jnp.where(sub == k, made[k], strip)
            if t == 0:
                strip = jnp.where(lane >= sub + q, strip, 0.0)
            emit(q, t, strip)
            upper[t].append(strip)
        before.append((q, inv, low, rows))
    end = first + TILE * group
    if end < LANES:
        done = jnp.concatenate([jnp.concatenate(u, axis=0) for u in upper], axis=1)
        a_ref[end:, :] -= stacked_dot(done[:, :LANES], done)[end:]


def early_kernel(
    n, m, rows, parts,
    f_hbm, o_hbm, k_hbm, r_hbm, fn_hbm, on_hbm, g_out, w_out, rp_out,
    f_ref, o_ref, k_ref, r_ref, fn_ref, on_ref, xlo, xhi, ylo, yhi, passing,
    local_sem, xs_sem, xr_sem, ys_sem, yr_sem, ps_sem, pr_sem, as_sem, ar_sem, *scratch
):
    i, j = lax.axis_index("gx"), lax.axis_index("gy")
    index = {"gx": i, "gy": j}
    planes, width, depth = f_ref.shape
    blocks = depth // LANES
    scratch = list(scratch)
    take = lambda count: [scratch.pop(0) for _ in range(count)]
    grams, inbox, held, inbox_x, held_x, inbox_z = (take(blocks) for _ in range(6))
    totals = take(blocks - 1) + [g_out]
    panels = take(blocks - 1)
    step = width // parts
    sides = (
        (i < n - 1, i > 0, i + 1, j),
        (i > 0, i < n - 1, i - 1, j),
        (j < m - 1, j > 0, i, j + 1),
        (j > 0, j < m - 1, i, j - 1),
    )
    z, odd, depth_z = i // 2, lax.rem(i, 2) == 1, n // 2
    rising = lambda pair: (pair + 1) * parts // depth_z
    falling = lambda pair: (depth_z - 1 - pair) * parts // depth_z
    if n % 2 or n < 4:
        indirect = (0, 0)
        relayed = 0
    else:
        indirect = (jnp.where(odd, falling(z), 0), jnp.where(odd, 0, rising(z - 1)))
        relayed = jnp.where(odd, rising(z - 1), falling(z))
    via = (i - 1, i + 1)
    onward = jnp.where(odd, i - 2, i + 2)
    lands = (jnp.logical_not(odd), odd)
    relayed = jnp.where(odd, jnp.where(z > 0, relayed, 0), jnp.where(z < depth_z - 1, relayed, 0))
    loads = [
        pltpu.make_async_copy(src, dst, local_sem.at[t])
        for t, (src, dst) in enumerate(((f_hbm, f_ref), (o_hbm, o_ref), (k_hbm, k_ref), (r_hbm, r_ref)))
    ]
    for copy in loads:
        copy.start()
    core, along = ("gy", 1, 2), ("gx", 2, n // 2)
    ring = [(i, peer(index, core, 1)[2][1])]
    ring += [peer(index, along, k)[2] for k in range(1, n // 2)]
    corners = [(i, peer(index, ("gy", 2, 2), 1)[2][1]), (peer(index, ("gx", 1, 2), 1)[2][0], j)]
    corners.append((corners[1][0], corners[0][1]))
    greets = sides + ((i < n - 2, None, i + 2, j), (i > 1, None, i - 2, j))
    barrier = pltpu.get_barrier_semaphore()
    greeted = sum(has.astype(jnp.int32) for has, _, _, _ in greets)
    for has, _, a, b in greets:
        @pl.when(has)
        def _(a=a, b=b):
            pl.semaphore_signal(barrier, inc=1, device_id=(a, b), device_id_type=MESH)
    for device in ring + corners:
        pl.semaphore_signal(barrier, inc=1, device_id=device, device_id_type=MESH)
        greeted = greeted + 1
    with jax.named_scope("barrier"):
        pl.semaphore_wait(barrier, greeted)
    fields = (f_hbm, o_hbm, k_hbm)

    def cut(at):
        c, q = divmod(at, parts)
        return pl.ds(q * step, step), pl.ds(c * LANES, LANES)

    def x_copies(side, at):
        _, _, a, b = sides[side]
        return [
            pltpu.make_async_remote_copy(
                src_ref=ref.at[((planes - 1, 0)[side],) + cut(at)],
                dst_ref=(xlo, xhi)[side].at[(t,) + cut(at)],
                send_sem=xs_sem.at[side],
                recv_sem=xr_sem.at[side, at],
                device_id=(a, b),
                device_id_type=MESH,
            )
            for t, ref in enumerate(fields)
        ]

    def to_relay(side, at):
        return [
            pltpu.make_async_remote_copy(
                src_ref=ref.at[((planes - 1, 0)[side],) + cut(at)],
                dst_ref=passing.at[(t,) + cut(at)],
                send_sem=xs_sem.at[side],
                recv_sem=pr_sem.at[at],
                device_id=(via[side], j),
                device_id_type=MESH,
            )
            for t, ref in enumerate(fields)
        ]

    def from_relay(side, at):
        return [
            pltpu.make_async_remote_copy(
                src_ref=passing.at[(t,) + cut(at)],
                dst_ref=(xlo, xhi)[side].at[(t,) + cut(at)],
                send_sem=ps_sem.at[0],
                recv_sem=xr_sem.at[side, at],
                device_id=(onward, j),
                device_id_type=MESH,
            )
            for t in range(3)
        ]

    def y_copies(side):
        _, _, a, b = sides[2 + side]
        return [
            pltpu.make_async_remote_copy(
                src_ref=ref.at[:, pl.ds((width - TILE, 0)[side], TILE)],
                dst_ref=(ylo, yhi)[side].at[t],
                send_sem=ys_sem.at[side],
                recv_sem=yr_sem.at[side],
                device_id=(a, b),
                device_id_type=MESH,
            )
            for t, ref in enumerate(fields)
        ]

    def whole(ref, send, recv, device=None):
        return pltpu.make_async_remote_copy(
            src_ref=ref, dst_ref=ref, send_sem=send, recv_sem=recv, device_id=device or (i, j), device_id_type=MESH
        )

    def post(at):
        q = at % parts
        for side in range(2):
            @pl.when(sides[side][0] & (q >= indirect[side]))
            def _(side=side):
                for copy in x_copies(side, at):
                    copy.start()

            @pl.when(sides[side][0] & (q < indirect[side]))
            def _(side=side):
                for copy in to_relay(side, at):
                    copy.start()

    row = lax.broadcasted_iota(jnp.int32, (step, LANES), 0)
    lane = lax.broadcasted_iota(jnp.int32, (step, LANES), 1)
    refs = (f_ref, o_ref, k_ref)
    zero = jnp.zeros((step, LANES), jnp.float32)
    zrow = jnp.zeros((1, LANES), jnp.float32)
    columns = (((0,), (0,)), ((), ()))
    products = (((1,), (0,)), ((), ()))

    def dot(left, right, dims):
        return lax.dot_general(left, right, dims, precision=HIGHEST, preferred_element_type=jnp.float32)

    def arrive(at):
        q = at % parts
        @pl.when(q < relayed)
        def _():
            whole(passing.at[(slice(None),) + cut(at)], ps_sem.at[0], pr_sem.at[at]).wait_recv()

        for side in range(2):
            @pl.when((q < relayed) & lands[side])
            def _(side=side):
                for copy in from_relay(side, at):
                    copy.start()

        for side in range(2):
            @pl.when(sides[side][1])
            def _(side=side):
                whole((xlo, xhi)[side].at[(slice(None),) + cut(at)], xs_sem.at[side], xr_sem.at[side, at]).wait_recv()

    def advance(at):
        c, q = divmod(at, parts)
        y = q * step
        here = cut(at)
        cols = here[1]
        for x in range(planes):
            center = [ref[(x,) + here] for ref in refs]
            sets = []
            if x == 0:
                sets.append([jnp.where(i > 0, xlo[(t,) + here], zero) for t in range(3)])
            else:
                sets.append([ref[(x - 1,) + here] for ref in refs])
            if x == planes - 1:
                sets.append([jnp.where(i < n - 1, xhi[(t,) + here], zero) for t in range(3)])
            else:
                sets.append([ref[(x + 1,) + here] for ref in refs])
            if y == 0:
                before = [jnp.where(j > 0, ylo[t, x, TILE - 1:TILE, cols], zrow) for t in range(3)]
            else:
                before = [ref[x, y - 1:y, cols] for ref in refs]
            if y + step == width:
                after = [jnp.where(j < m - 1, yhi[t, x, 0:1, cols], zrow) for t in range(3)]
            else:
                after = [ref[x, y + step:y + step + 1, cols] for ref in refs]
            sets.append([jnp.where(row == 0, b, pltpu.roll(v, 1, 0)) for b, v in zip(before, center)])
            sets.append([jnp.where(row == step - 1, a, pltpu.roll(v, step - 1, 0)) for a, v in zip(after, center)])
            if c:
                left = [pltpu.roll(ref[x, here[0], pl.ds((c - 1) * LANES, LANES)], 1, 1) for ref in refs]
            else:
                left = [zero] * 3
            if c < blocks - 1:
                right = [pltpu.roll(ref[x, here[0], pl.ds((c + 1) * LANES, LANES)], LANES - 1, 1) for ref in refs]
            else:
                right = [zero] * 3
            sets.append([jnp.where(lane == 0, b, pltpu.roll(v, 1, 1)) for b, v in zip(left, center)])
            sets.append([jnp.where(lane == LANES - 1, a, pltpu.roll(v, LANES - 1, 1)) for a, v in zip(right, center)])
            fc, oc, kc = center
            df, do = zero, zero
            for fs, os, ks in sets:
                weight = 0.5 * (kc + ks)
                df = df + weight * (fs - fc)
                do = do + weight * (os - oc)
            prod = fc * oc
            react = r_ref[(x,) + here] * prod / jnp.sqrt(1.0 + prod * prod)
            fn_ref[(x,) + here] = fc + 0.15 * (df - react)
            on_ref[(x,) + here] = oc + 0.15 * (do + react)
        to = (c + 1) * LANES
        u = jnp.concatenate([ref[x, here[0], :to] for ref in (fn_ref, on_ref) for x in range(planes)], axis=0)
        total = dot(u, u[:, c * LANES:], columns)
        grams[c][...] = total if q == 0 else grams[c][...] + total

    def sends(c, s, source, target, devices):
        return [
            pltpu.make_async_remote_copy(
                src_ref=source(*to),
                dst_ref=target(*to),
                send_sem=as_sem.at[c, s],
                recv_sem=ar_sem.at[c, s],
                device_id=device,
                device_id_type=MESH,
            )
            for to, device in devices
        ]

    def span(at, length):
        return pl.ds(pl.multiple_of(at * length, TILE), length)

    half = [(c + 1) * LANES // 2 for c in range(blocks)]
    piece = [length // (n // 2) for length in half]
    mine_core, mine_along = lax.rem(j, 2), i // 2
    beside = [((1 - mine_core, 0), ring[0])]
    others = [((lax.rem(mine_along + k, n // 2), k - 1), ring[k]) for k in range(1, n // 2)]
    around = [((0, k), corners[k]) for k in range(3)]

    def whole_slot(c):
        start = mine_core * half[c] + mine_along * piece[c]
        return pl.ds(pl.multiple_of(start, TILE), piece[c])

    def exchange(c, s):
        if s == 0:
            return sends(c, 0, lambda a, k: grams[c].at[span(a, half[c])], lambda a, k: inbox[c], beside)
        if s == 1:
            return sends(c, 1, lambda a, k: held[c].at[span(a, piece[c])], lambda a, k: inbox_x[c].at[k], others)
        if s == 2:
            return sends(c, 2, lambda a, k: held_x[c], lambda a, k: inbox_z[c].at[k], around)
        if s == 3:
            slot = whole_slot(c)
            return sends(c, 3, lambda a, k: totals[c].at[slot], lambda a, k: totals[c].at[slot], others)
        part = span(mine_core, half[c])
        return sends(c, 4, lambda a, k: totals[c].at[part], lambda a, k: totals[c].at[part], beside)

    def landed(c, s):
        region = (inbox[c], inbox_x[c], inbox_z[c], inbox_x[c], inbox[c])[s]
        return whole(region, as_sem.at[c, s], ar_sem.at[c, s])

    def reduce_step(c, s):
        if s:
            landed(c, s - 1).wait_recv()
        if s == 1:
            held[c][...] = grams[c][span(mine_core, half[c])] + inbox[c][...]
        if s == 2:
            total = held[c][span(mine_along, piece[c])]
            for k in range(n // 2 - 1):
                total = total + inbox_x[c][k]
            held_x[c][...] = total
        if s == 3:
            total = (held_x[c][...] + inbox_z[c][0]) + (inbox_z[c][1] + inbox_z[c][2])
            totals[c][whole_slot(c)] = total / rows
        if s < 5:
            for copy in exchange(c, s):
                copy.start()

    eye = jnp.where(
        lax.broadcasted_iota(jnp.int32, (LANES, LANES), 0) == lax.broadcasted_iota(jnp.int32, (LANES, LANES), 1), 1.0, 0.0
    )

    def prepare(b):
        c0 = b * LANES
        panel, total = panels[b], totals[b]
        s = total[c0:c0 + LANES]
        if b:
            above = dot(w_out[:c0, :c0], total[:c0], products)
            rp_out[:c0, c0:c0 + LANES] = above
            s = s - dot(above, above, columns)
            panel[:, LANES:c0 + LANES] = -dot(above, w_out[:c0, :c0], columns)
        panel[:, :LANES] = s
        panel[:, c0 + LANES:] = eye
        if c0:
            rp_out[c0:c0 + LANES, :c0] = jnp.zeros((LANES, c0), jnp.float32)
        rest = w_out.shape[1] - c0 - LANES
        if rest:
            w_out[c0:c0 + LANES, c0 + LANES:] = jnp.zeros((LANES, rest), jnp.float32)

    def pivot(b, g):
        c0 = b * LANES

        def emit(q, t, strip):
            at = slice(c0 + q, c0 + q + TILE)
            if t == 0:
                rp_out[at, c0:c0 + LANES] = strip
            else:
                w_out[at, (t - 1) * LANES:t * LANES] = strip

        eliminate(panels[b], GROUP, g * GROUP * TILE, emit)

    steps = blocks * parts
    groups = LANES // (TILE * GROUP)
    R = lambda c, s: functools.partial(reduce_step, c, s)
    prep = lambda b: functools.partial(prepare, b)
    C = lambda b, g: functools.partial(pivot, b, g)
    plan = {}
    if blocks == 3 and parts == 4 and groups == 4:
        plan = {
            3: [R(0, 0)], 4: [R(0, 1)], 6: [R(0, 2)], 7: [R(1, 0)], 8: [R(1, 1)], 9: [R(0, 3)], 10: [R(1, 2)],
            11: [
                R(2, 0), R(0, 4), R(1, 3), R(2, 1), R(0, 5), prep(0), C(0, 0), C(0, 1), C(0, 2), R(1, 4), R(2, 2), C(0, 3),
                R(1, 5), prep(1), C(1, 0), R(2, 3), C(1, 1), C(1, 2), C(1, 3), R(2, 4), R(2, 5),
            ],
        }
    else:
        last = []
        for c in range(blocks):
            last += [R(c, s) for s in range(6)]
            if c < blocks - 1:
                last += [prep(c)] + [C(c, g) for g in range(groups)]
        plan = {steps - 1: last}
    for side in range(2):
        @pl.when(sides[2 + side][0])
        def _(side=side):
            for copy in y_copies(side):
                copy.start()
    for at in range(min(AHEAD, steps)):
        post(at)
    for copy in loads:
        copy.wait()
    for side in range(2):
        @pl.when(sides[2 + side][1])
        def _(side=side):
            whole((ylo, yhi)[side], ys_sem.at[side], yr_sem.at[side]).wait_recv()
    stores = [
        pltpu.make_async_copy(src, dst, local_sem.at[t])
        for t, (src, dst) in enumerate(((fn_ref, fn_hbm), (on_ref, on_hbm)))
    ]
    for at in range(steps):
        with jax.named_scope(f"w{at}"):
            arrive(at)
        if at + AHEAD < steps:
            post(at + AHEAD)
        with jax.named_scope(f"s{at}"):
            advance(at)
        for task in plan.get(at, []):
            name = {"reduce_step": "R", "prepare": "P", "pivot": "C"}[task.func.__name__]
            with jax.named_scope(name + "".join(map(str, task.args))):
                task()
            if at == steps - 1 and task is plan[at][0]:
                for copy in stores:
                    copy.start()
    with jax.named_scope("sends"):
        for c in range(blocks):
            for s in range(5):
                landed(c, s).wait_send()
        for side in range(2):
            @pl.when(sides[2 + side][0])
            def _(side=side):
                whole((ylo, yhi)[side], ys_sem.at[side], yr_sem.at[side]).wait_send()

            @pl.when(sides[side][0])
            def _(side=side):
                whole((xlo, xhi)[side], xs_sem.at[side], xr_sem.at[side, 0]).wait_send()

        for count in range(1, parts):
            @pl.when(relayed == count)
            def _(count=count):
                whole(passing.at[:, pl.ds(0, count * step)], ps_sem.at[0], pr_sem.at[0]).wait_send()
        for copy in stores:
            copy.wait()


def early(n, m, rows, fuel, oxidizer, kappa, rate):
    planes, width, depth = fuel.shape
    blocks = depth // LANES
    parts = 4 if width % (4 * TILE) == 0 else 1
    steps = blocks * parts
    size = [(c + 1) * LANES for c in range(blocks)]
    vmem = lambda *shape: pltpu.VMEM(shape, jnp.float32)
    inner = depth - LANES
    scratch = [vmem(*fuel.shape)] * 6
    scratch += [vmem(3, width, depth)] * 2
    scratch += [vmem(3, planes, TILE, depth)] * 2
    scratch += [vmem(3, width, depth)]
    scratch += [pltpu.SemaphoreType.DMA((4,))]
    scratch += [pltpu.SemaphoreType.DMA((2,)), pltpu.SemaphoreType.DMA((2, steps))]
    scratch += [pltpu.SemaphoreType.DMA((2,))] * 2
    scratch += [pltpu.SemaphoreType.DMA((1,)), pltpu.SemaphoreType.DMA((steps,))]
    scratch += [pltpu.SemaphoreType.DMA((blocks, 5))] * 2
    scratch += [vmem(length, LANES) for length in size]
    scratch += [vmem(length // 2, LANES) for length in size] * 2
    scratch += [vmem(n // 2 - 1, length // n, LANES) for length in size]
    scratch += [vmem(length // n, LANES) for length in size]
    scratch += [vmem(3, length // n, LANES) for length in size]
    scratch += [vmem(length, LANES) for length in size[:-1]]
    scratch += [vmem(LANES, (b + 2) * LANES) for b in range(blocks - 1)]
    field = jax.ShapeDtypeStruct(fuel.shape, jnp.float32)
    any_spec = pl.BlockSpec(memory_space=pl.ANY)
    vmem_spec = pl.BlockSpec(memory_space=pltpu.VMEM)
    return pl.pallas_call(
        functools.partial(early_kernel, n, m, rows, parts),
        out_shape=(field, field, vmem(depth, LANES), vmem(inner, inner), vmem(inner, inner)),
        in_specs=[any_spec] * 4,
        out_specs=(any_spec, any_spec, vmem_spec, vmem_spec, vmem_spec),
        scratch_shapes=scratch,
        compiler_params=pltpu.CompilerParams(collective_id=0, has_side_effects=True),
        name="early",
    )(fuel, oxidizer, kappa, rate)


def finish_kernel(g_ref, w_ref, rp_ref, fn_in, on_in, r_ref, fn_out, on_out, a_ref, fn_ref, on_ref, sems):
    loads = [pltpu.make_async_copy(fn_in, fn_ref, sems.at[0]), pltpu.make_async_copy(on_in, on_ref, sems.at[1])]
    stores = [pltpu.make_async_copy(fn_ref, fn_out, sems.at[2]), pltpu.make_async_copy(on_ref, on_out, sems.at[3])]
    for copy in loads:
        copy.start()
    inner = w_ref.shape[0]
    dot = functools.partial(lax.dot_general, precision=HIGHEST, preferred_element_type=jnp.float32)
    above = dot(w_ref[...], g_ref[:inner], (((1,), (0,)), ((), ())))
    a_ref[...] = g_ref[inner:] - dot(above, above, (((0,), (0,)), ((), ())))
    r_ref[:inner, :inner] = rp_ref[...]
    r_ref[:inner, inner:] = above
    r_ref[inner:, :inner] = jnp.zeros((LANES, inner), jnp.float32)

    def emit(q, t, strip):
        r_ref[inner + q:inner + q + TILE, inner:] = strip

    for first in range(0, LANES, GROUP * TILE):
        eliminate(a_ref, GROUP, first, emit)
        if first == 0:
            for load, store in zip(loads, stores):
                load.wait()
                store.start()
    for copy in stores:
        copy.wait()


def finish(gram, inverse, upper, fuel_next, oxid_next):
    depth = fuel_next.shape[2]
    field = jax.ShapeDtypeStruct(fuel_next.shape, jnp.float32)
    vmem = pl.BlockSpec(memory_space=pltpu.VMEM)
    any_spec = pl.BlockSpec(memory_space=pl.ANY)
    gram, inverse, upper = (pltpu.with_memory_space_constraint(v, pltpu.VMEM) for v in (gram, inverse, upper))
    return pl.pallas_call(
        finish_kernel,
        out_shape=(jax.ShapeDtypeStruct((depth, depth), jnp.float32), field, field),
        in_specs=[vmem, vmem, vmem, any_spec, any_spec],
        out_specs=(vmem, any_spec, any_spec),
        scratch_shapes=[
            pltpu.VMEM((LANES, LANES), jnp.float32),
            pltpu.VMEM(fuel_next.shape, jnp.float32),
            pltpu.VMEM(fuel_next.shape, jnp.float32),
            pltpu.SemaphoreType.DMA((4,)),
        ],
        name="finish",
    )(gram, inverse, upper, fuel_next, oxid_next)


def stacked_dot(left, right):
    dims = (((0,), (0,)), ((), ()))
    def pieces(v):
        h = v.astype(jnp.bfloat16).astype(jnp.float32)
        m = (v - h).astype(jnp.bfloat16).astype(jnp.float32)
        return h, m, v - h - m
    (a, b, c), (d, e, f) = pieces(left), pieces(right)
    lhs = jnp.concatenate([a, a, b, a, c, b], axis=0).astype(jnp.bfloat16)
    rhs = jnp.concatenate([d, e, d, f, d, e], axis=0).astype(jnp.bfloat16)
    return lax.dot_general(lhs, rhs, dims, preferred_element_type=jnp.float32)


def column_of(panel, at):
    return jnp.broadcast_to(panel[:, at:at + 1], (TILE, LANES))


def factor_kernel(group, g_ref, fn_in, on_in, r_ref, fn_out, on_out, a_ref, fn_ref, on_ref, sems):
    loads = [pltpu.make_async_copy(fn_in, fn_ref, sems.at[0]), pltpu.make_async_copy(on_in, on_ref, sems.at[1])]
    stores = [pltpu.make_async_copy(fn_ref, fn_out, sems.at[2]), pltpu.make_async_copy(on_ref, on_out, sems.at[3])]
    for copy in loads:
        copy.start()
    depth = r_ref.shape[0]
    blocks = depth // LANES
    at = 0
    for b in range(blocks):
        for c in range(b, blocks):
            a_ref[b * LANES:(b + 1) * LANES, c * LANES:(c + 1) * LANES] = g_ref[at:at + LANES]
            at += LANES
    dims = (((0,), (0,)), ((), ()))
    dot = functools.partial(lax.dot_general, dimension_numbers=dims, precision=HIGHEST, preferred_element_type=jnp.float32)
    sub = lax.broadcasted_iota(jnp.int32, (TILE, LANES), 0)
    lane = lax.broadcasted_iota(jnp.int32, (TILE, LANES), 1)
    for b in range(blocks):
        c0 = b * LANES
        tiles = range(blocks - b)
        if c0:
            r_ref[c0:c0 + LANES, :c0] = jnp.zeros((LANES, c0), jnp.float32)
        for p in range(0, LANES, TILE * group):
            before = []
            for q in range(p, p + TILE * group, TILE):
                r0 = c0 + q
                strips = [a_ref[r0:r0 + TILE, c0 + t * LANES:c0 + (t + 1) * LANES] for t in tiles]
                for s, inv, low, rows in before:
                    factors = []
                    for k in range(TILE):
                        value = column_of(strips[0], s + k)
                        for j in range(k):
                            value = value - factors[j] * low[k, j]
                        factors.append(value * inv[k])
                    for t in tiles:
                        for k in range(TILE):
                            strips[t] = strips[t] - factors[k] * rows[t][k]
                e = {}
                for k in range(TILE):
                    column = column_of(strips[0], q + k)
                    for i in range(k, TILE):
                        e[i, k] = jnp.broadcast_to(column[i:i + 1], (TILE, LANES))
                inv, low = [], {}
                for k in range(TILE):
                    inv.append(lax.rsqrt(e[k, k]))
                    for i in range(k + 1, TILE):
                        low[i, k] = e[i, k] * inv[k]
                    for j in range(k + 1, TILE):
                        for i in range(j, TILE):
                            e[i, j] = e[i, j] - low[i, k] * low[j, k]
                rows = []
                for t in tiles:
                    made = []
                    for k in range(TILE):
                        value = jnp.broadcast_to(strips[t][k:k + 1], (TILE, LANES))
                        for j in range(k):
                            value = value - low[k, j] * made[j]
                        made.append(value * inv[k])
                    rows.append(made)
                    strip = made[0]
                    for k in range(1, TILE):
                        strip = jnp.where(sub == k, made[k], strip)
                    if t == 0:
                        strip = jnp.where(lane >= sub + q, strip, 0.0)
                    r_ref[r0:r0 + TILE, c0 + t * LANES:c0 + (t + 1) * LANES] = strip
                before.append((q, inv, low, rows))
            low_end = p + TILE * group
            if low_end < LANES:
                upper = r_ref[c0 + p:c0 + low_end, c0:]
                a_ref[c0 + low_end:c0 + LANES, c0:] -= stacked_dot(upper[:, :LANES], upper)[low_end:]
        if b == 0:
            for load, store in zip(loads, stores):
                load.wait()
                store.start()
        for d in range(b + 1, blocks):
            d0 = d * LANES
            a_ref[d0:d0 + LANES, d0:] -= dot(r_ref[c0:c0 + LANES, d0:d0 + LANES], r_ref[c0:c0 + LANES, d0:])
    for copy in stores:
        copy.wait()


def factor(gram, fuel_next, oxid_next):
    depth = fuel_next.shape[2]
    field = jax.ShapeDtypeStruct(fuel_next.shape, jnp.float32)
    vmem = pl.BlockSpec(memory_space=pltpu.VMEM)
    any_spec = pl.BlockSpec(memory_space=pl.ANY)
    return pl.pallas_call(
        functools.partial(factor_kernel, 4),
        out_shape=(jax.ShapeDtypeStruct((depth, depth), jnp.float32), field, field),
        in_specs=[vmem, any_spec, any_spec],
        out_specs=(vmem, any_spec, any_spec),
        scratch_shapes=[
            pltpu.VMEM((depth, depth), jnp.float32),
            pltpu.VMEM(fuel_next.shape, jnp.float32),
            pltpu.VMEM(fuel_next.shape, jnp.float32),
            pltpu.SemaphoreType.DMA((4,)),
        ],
        name="factor",
    )(gram, fuel_next, oxid_next)


def shards(n, m, fuel, oxidizer, kappa, rate):
    planes, width, depth = fuel.shape
    rows = 2 * planes * width * n * m
    blocks = depth // LANES
    if blocks > 1 and m == 4 and n % 2 == 0 and n >= 4 and LANES % (TILE * n) == 0:
        fuel_next, oxid_next, gram, inverse, upper = early(n, m, rows, fuel, oxidizer, kappa, rate)
        r_factor, fuel_next, oxid_next = finish(gram, inverse, upper, fuel_next, oxid_next)
        return (fuel_next, oxid_next, r_factor)
    fuel_next, oxid_next, gram = update(n, m, rows, (), fuel, oxidizer, kappa, rate)
    gram = lax.psum(gram, ("gx", "gy"))
    r_factor, fuel_next, oxid_next = factor(gram, fuel_next, oxid_next)
    return (fuel_next, oxid_next, r_factor)


def solution(mesh):
    spec = P("gx", "gy", None)
    body = functools.partial(shards, mesh.shape["gx"], mesh.shape["gy"])
    return jax.shard_map(body, mesh=mesh, in_specs=(spec,) * 4, out_specs=(spec, spec, P()), check_vma=False)
```

```python
import functools

import jax
import jax.numpy as jnp
from jax import lax
from jax.experimental import pallas as pl
from jax.experimental.pallas import tpu as pltpu
from jax.sharding import PartitionSpec as P

MESH = pl.DeviceIdType.MESH
TILE = 8
LANES = 128
HIGHEST = lax.Precision.HIGHEST
GROUP = 4
AHEAD = 3
LEAD = 2


def peer(index, stage, k):
    axis, stride, size = stage
    mine = lax.rem(index[axis] // stride, size)
    other = lax.rem(mine + k, size)
    place = dict(index)
    place[axis] = index[axis] + (other - mine) * stride
    return mine, other, (place["gx"], place["gy"])


def sum_over_all(index, stages, source, out_ref, inbox, held, sems):
    count = len(stages)
    length = source.shape[0]
    starts = []
    start = 0
    for s, stage in enumerate(stages):
        size = stage[2]
        length //= size
        sent = []
        for k in range(1, size):
            mine, other, device = peer(index, stage, k)
            sent.append(
                pltpu.make_async_remote_copy(
                    src_ref=source.at[pl.ds(pl.multiple_of(other * length, TILE), length)],
                    dst_ref=inbox[s].at[k - 1],
                    send_sem=sems[0].at[s, k - 1],
                    recv_sem=sems[1].at[s, k - 1],
                    device_id=device,
                    device_id_type=MESH,
                )
            )
            sent[-1].start()
        for copy in sent:
            copy.wait_recv()
        total = source[pl.ds(pl.multiple_of(mine * length, TILE), length)]
        for k in range(1, size):
            total = total + inbox[s][k - 1]
        held[s][...] = total
        for copy in sent:
            copy.wait_send()
        source = held[s]
        start = start + mine * length
        starts.append((start, length))
    part = pl.ds(pl.multiple_of(start, TILE), length)
    out_ref[part] = source[...]
    for s in reversed(range(count)):
        start, length = starts[s]
        part = pl.ds(pl.multiple_of(start, TILE), length)
        sent = []
        for k in range(1, stages[s][2]):
            sent.append(
                pltpu.make_async_remote_copy(
                    src_ref=out_ref.at[part],
                    dst_ref=out_ref.at[part],
                    send_sem=sems[2].at[s, k - 1],
                    recv_sem=sems[3].at[s, k - 1],
                    device_id=peer(index, stages[s], k)[2],
                    device_id_type=MESH,
                )
            )
            sent[-1].start()
        for copy in sent:
            copy.wait()


def update_kernel(
    n, m, rows, parts, stages,
    f_hbm, o_hbm, k_hbm, r_hbm, fn_hbm, on_hbm, g_out,
    f_ref, o_ref, k_ref, r_ref, fn_ref, on_ref, xlo, xhi, ylo, yhi, gram, passing,
    local_sem, xs_sem, xr_sem, ys_sem, yr_sem, ps_sem, pr_sem, *scratch
):
    i, j = lax.axis_index("gx"), lax.axis_index("gy")
    index = {"gx": i, "gy": j}
    planes, width, depth = f_ref.shape
    step = width // parts
    sides = (
        (i < n - 1, i > 0, i + 1, j),
        (i > 0, i < n - 1, i - 1, j),
        (j < m - 1, j > 0, i, j + 1),
        (j > 0, j < m - 1, i, j - 1),
    )
    z, odd, depth_z = i // 2, lax.rem(i, 2) == 1, n // 2
    rising = lambda pair: (pair + 1) * parts // depth_z
    falling = lambda pair: (depth_z - 1 - pair) * parts // depth_z
    if n % 2 or n < 4:
        indirect = (0, 0)
        relayed = 0
    else:
        indirect = (jnp.where(odd, falling(z), 0), jnp.where(odd, 0, rising(z - 1)))
        relayed = jnp.where(odd, rising(z - 1), falling(z))
    via = (i - 1, i + 1)
    onward = jnp.where(odd, i - 2, i + 2)
    lands = (jnp.logical_not(odd), odd)
    relayed = jnp.where(odd, jnp.where(z > 0, relayed, 0), jnp.where(z < depth_z - 1, relayed, 0))
    greets = sides + ((i < n - 2, None, i + 2, j), (i > 1, None, i - 2, j))
    barrier = pltpu.get_barrier_semaphore()
    greeted = sum(has.astype(jnp.int32) for has, _, _, _ in greets)
    for has, _, a, b in greets:
        @pl.when(has)
        def _(a=a, b=b):
            pl.semaphore_signal(barrier, inc=1, device_id=(a, b), device_id_type=MESH)
    for stage in stages:
        for k in range(1, stage[2]):
            pl.semaphore_signal(barrier, inc=1, device_id=peer(index, stage, k)[2], device_id_type=MESH)
            greeted = greeted + 1
    pl.semaphore_wait(barrier, greeted)
    fields = (f_hbm, o_hbm, k_hbm)

    def x_copies(side, part):
        _, _, a, b = sides[side]
        cut = pl.ds(part * step, step)
        return [
            pltpu.make_async_remote_copy(
                src_ref=ref.at[(planes - 1, 0)[side], cut],
                dst_ref=(xlo, xhi)[side].at[t, cut],
                send_sem=xs_sem.at[side, part, t],
                recv_sem=xr_sem.at[side, part, t],
                device_id=(a, b),
                device_id_type=MESH,
            )
            for t, ref in enumerate(fields)
        ]

    def to_relay(side, part):
        cut = pl.ds(part * step, step)
        return [
            pltpu.make_async_remote_copy(
                src_ref=ref.at[(planes - 1, 0)[side], cut],
                dst_ref=passing.at[t, cut],
                send_sem=xs_sem.at[side, part, t],
                recv_sem=pr_sem.at[part, t],
                device_id=(via[side], j),
                device_id_type=MESH,
            )
            for t, ref in enumerate(fields)
        ]

    def from_relay(side, part):
        cut = pl.ds(part * step, step)
        return [
            pltpu.make_async_remote_copy(
                src_ref=passing.at[t, cut],
                dst_ref=(xlo, xhi)[side].at[t, cut],
                send_sem=ps_sem.at[part, t],
                recv_sem=xr_sem.at[side, part, t],
                device_id=(onward, j),
                device_id_type=MESH,
            )
            for t in range(3)
        ]

    def y_copies(side):
        _, _, a, b = sides[2 + side]
        return [
            pltpu.make_async_remote_copy(
                src_ref=ref.at[:, pl.ds((width - TILE, 0)[side], TILE)],
                dst_ref=(ylo, yhi)[side].at[t],
                send_sem=ys_sem.at[side, t],
                recv_sem=yr_sem.at[side, t],
                device_id=(a, b),
                device_id_type=MESH,
            )
            for t, ref in enumerate(fields)
        ]

    for side in range(2):
        @pl.when(sides[2 + side][0])
        def _(side=side):
            for copy in y_copies(side):
                copy.start()
    for part in range(parts):
        for side in range(2):
            @pl.when(sides[side][0] & (part >= indirect[side]))
            def _(side=side, part=part):
                for copy in x_copies(side, part):
                    copy.start()

            @pl.when(sides[side][0] & (part < indirect[side]))
            def _(side=side, part=part):
                for copy in to_relay(side, part):
                    copy.start()
    loads = [
        pltpu.make_async_copy(src, dst, local_sem.at[t])
        for t, (src, dst) in enumerate(((f_hbm, f_ref), (o_hbm, o_ref), (k_hbm, k_ref), (r_hbm, r_ref)))
    ]
    for copy in loads:
        copy.start()
    for copy in loads:
        copy.wait()
    for side in range(2):
        @pl.when(sides[2 + side][1])
        def _(side=side):
            for copy in y_copies(side):
                copy.wait_recv()

    row = lax.broadcasted_iota(jnp.int32, (step, depth), 0)
    lane = lax.broadcasted_iota(jnp.int32, (step, depth), 1)
    refs = (f_ref, o_ref, k_ref)
    zero = jnp.zeros((step, depth), jnp.float32)
    zrow = jnp.zeros((1, depth), jnp.float32)
    dims = (((0,), (0,)), ((), ()))
    for q in range(parts):
        @pl.when(q < relayed)
        def _(q=q):
            for copy in to_relay(0, q):
                copy.wait_recv()

        for side in range(2):
            @pl.when((q < relayed) & lands[side])
            def _(side=side, q=q):
                for copy in from_relay(side, q):
                    copy.start()

        for side in range(2):
            @pl.when(sides[side][1])
            def _(side=side, q=q):
                for copy in x_copies(side, q):
                    copy.wait_recv()
        y = q * step
        part = pl.ds(y, step)
        for x in range(planes):
            center = [ref[x, part] for ref in refs]
            sets = []
            if x == 0:
                sets.append([jnp.where(i > 0, xlo[t, part], zero) for t in range(3)])
            else:
                sets.append([ref[x - 1, part] for ref in refs])
            if x == planes - 1:
                sets.append([jnp.where(i < n - 1, xhi[t, part], zero) for t in range(3)])
            else:
                sets.append([ref[x + 1, part] for ref in refs])
            if y == 0:
                before = [jnp.where(j > 0, ylo[t, x, TILE - 1:TILE], zrow) for t in range(3)]
            else:
                before = [ref[x, y - 1:y] for ref in refs]
            if y + step == width:
                after = [jnp.where(j < m - 1, yhi[t, x, 0:1], zrow) for t in range(3)]
            else:
                after = [ref[x, y + step:y + step + 1] for ref in refs]
            sets.append([jnp.where(row == 0, b, pltpu.roll(c, 1, 0)) for b, c in zip(before, center)])
            sets.append([jnp.where(row == step - 1, a, pltpu.roll(c, step - 1, 0)) for a, c in zip(after, center)])
            sets.append([jnp.where(lane == 0, 0.0, pltpu.roll(c, 1, 1)) for c in center])
            sets.append([jnp.where(lane == depth - 1, 0.0, pltpu.roll(c, depth - 1, 1)) for c in center])
            fc, oc, kc = center
            df, do = zero, zero
            for fs, os, ks in sets:
                weight = 0.5 * (kc + ks)
                df = df + weight * (fs - fc)
                do = do + weight * (os - oc)
            prod = fc * oc
            react = r_ref[x, part] * prod / jnp.sqrt(1.0 + prod * prod)
            fn_ref[x, part] = fc + 0.15 * (df - react)
            on_ref[x, part] = oc + 0.15 * (do + react)
        u = jnp.concatenate([ref[x, part] for ref in (fn_ref, on_ref) for x in range(planes)], axis=0)
        at = 0
        for a in range(0, depth, LANES):
            total = lax.dot_general(u[:, a:a + LANES], u[:, a:], dims, precision=HIGHEST, preferred_element_type=jnp.float32)
            for b in range(0, depth - a, LANES):
                block = total[:, b:b + LANES]
                held_rows = slice(at, at + LANES)
                gram[held_rows] = block if q == 0 else gram[held_rows] + block
                at += LANES
    stores = [
        pltpu.make_async_copy(src, dst, local_sem.at[t])
        for t, (src, dst) in enumerate(((fn_ref, fn_hbm), (on_ref, on_hbm)))
    ]
    for copy in stores:
        copy.start()
    gram[...] = gram[...] / rows
    if stages:
        count = len(stages)
        sum_over_all(index, stages, gram, g_out, scratch[:count], scratch[count:2 * count], scratch[2 * count:])
    else:
        g_out[...] = gram[...]
    for side in range(2):
        @pl.when(sides[2 + side][0])
        def _(side=side):
            for copy in y_copies(side):
                copy.wait_send()

        @pl.when(sides[side][0])
        def _(side=side):
            for part in range(parts):
                for copy in x_copies(side, part):
                    copy.wait_send()

    for part in range(parts):
        @pl.when(part < relayed)
        def _(part=part):
            for copy in from_relay(0, part):
                copy.wait_send()
    for copy in stores:
        copy.wait()


def update(n, m, rows, stages, fuel, oxidizer, kappa, rate):
    planes, width, depth = fuel.shape
    blocks = depth // LANES
    parts = 4 if width % (4 * TILE) == 0 else 1
    gram_rows = blocks * (blocks + 1) // 2 * LANES
    scratch = [pltpu.VMEM(fuel.shape, jnp.float32)] * 6
    scratch += [pltpu.VMEM((3, width, depth), jnp.float32)] * 2
    scratch += [pltpu.VMEM((3, planes, TILE, depth), jnp.float32)] * 2
    scratch += [pltpu.VMEM((gram_rows, LANES), jnp.float32)]
    scratch += [pltpu.VMEM((3, width, depth), jnp.float32)]
    scratch += [pltpu.SemaphoreType.DMA((4,))]
    scratch += [pltpu.SemaphoreType.DMA((2, parts, 3))] * 2
    scratch += [pltpu.SemaphoreType.DMA((2, 3))] * 2
    scratch += [pltpu.SemaphoreType.DMA((parts, 3))] * 2
    if stages:
        inbox, held, length = [], [], gram_rows
        for _, _, size in stages:
            length //= size
            inbox.append(pltpu.VMEM((size - 1, length, LANES), jnp.float32))
            held.append(pltpu.VMEM((length, LANES), jnp.float32))
        most = max(stage[2] for stage in stages)
        scratch += inbox + held + [pltpu.SemaphoreType.DMA((len(stages), most - 1))] * 4
    field = jax.ShapeDtypeStruct(fuel.shape, jnp.float32)
    any_spec = pl.BlockSpec(memory_space=pl.ANY)
    return pl.pallas_call(
        functools.partial(update_kernel, n, m, rows, parts, stages),
        out_shape=(field, field, jax.ShapeDtypeStruct((gram_rows, LANES), jnp.float32)),
        in_specs=[any_spec] * 4,
        out_specs=(any_spec, any_spec, pl.BlockSpec(memory_space=pltpu.VMEM)),
        scratch_shapes=scratch,
        compiler_params=pltpu.CompilerParams(collective_id=0, has_side_effects=True),
        name="update",
    )(fuel, oxidizer, kappa, rate)


def eliminate(a_ref, group, first, emit):
    width = a_ref.shape[1]
    tiles = range(width // LANES)
    sub = lax.broadcasted_iota(jnp.int32, (TILE, LANES), 0)
    lane = lax.broadcasted_iota(jnp.int32, (TILE, LANES), 1)
    before, upper = [], [[] for _ in tiles]
    for q in range(first, first + TILE * group, TILE):
        strips = [a_ref[q:q + TILE, t * LANES:(t + 1) * LANES] for t in tiles]
        for s, inv, low, rows in before:
            factors = []
            for k in range(TILE):
                value = column_of(strips[0], s + k)
                for j in range(k):
                    value = value - factors[j] * low[k, j]
                factors.append(value * inv[k])
            for t in tiles:
                for k in range(TILE):
                    strips[t] = strips[t] - factors[k] * rows[t][k]
        e = {}
        for k in range(TILE):
            column = column_of(strips[0], q + k)
            for i in range(k, TILE):
                e[i, k] = jnp.broadcast_to(column[i:i + 1], (TILE, LANES))
        inv, low = [], {}
        for k in range(TILE):
            inv.append(lax.rsqrt(e[k, k]))
            for i in range(k + 1, TILE):
                low[i, k] = e[i, k] * inv[k]
            for j in range(k + 1, TILE):
                for i in range(j, TILE):
                    e[i, j] = e[i, j] - low[i, k] * low[j, k]
        rows = []
        for t in tiles:
            made = []
            for k in range(TILE):
                value = jnp.broadcast_to(strips[t][k:k + 1], (TILE, LANES))
                for j in range(k):
                    value = value - low[k, j] * made[j]
                made.append(value * inv[k])
            rows.append(made)
            strip = made[0]
            for k in range(1, TILE):
                strip = jnp.where(sub == k, made[k], strip)
            if t == 0:
                strip = jnp.where(lane >= sub + q, strip, 0.0)
            emit(q, t, strip)
            upper[t].append(strip)
        before.append((q, inv, low, rows))
    end = first + TILE * group
    if end < LANES:
        done = jnp.concatenate([jnp.concatenate(u, axis=0) for u in upper], axis=1)
        a_ref[end:, :] -= stacked_dot(done[:, :LANES], done)[end:]


def early_kernel(
    n, m, rows, parts,
    f_hbm, o_hbm, k_hbm, r_hbm, fn_hbm, on_hbm, g_out, w_out, rp_out,
    f_ref, o_ref, k_ref, r_ref, fn_ref, on_ref, xlo, xhi, ylo, yhi, passing,
    local_sem, xs_sem, xr_sem, ys_sem, yr_sem, ps_sem, pr_sem, as_sem, ar_sem, *scratch
):
    i, j = lax.axis_index("gx"), lax.axis_index("gy")
    index = {"gx": i, "gy": j}
    planes, width, depth = f_ref.shape
    blocks = depth // LANES
    scratch = list(scratch)
    take = lambda count: [scratch.pop(0) for _ in range(count)]
    grams, inbox, held, inbox_x, held_x, inbox_z = (take(blocks) for _ in range(6))
    totals = take(blocks - 1) + [g_out]
    panels = take(blocks - 1)
    step = width // parts
    sides = (
        (i < n - 1, i > 0, i + 1, j),
        (i > 0, i < n - 1, i - 1, j),
        (j < m - 1, j > 0, i, j + 1),
        (j > 0, j < m - 1, i, j - 1),
    )
    z, odd, depth_z = i // 2, lax.rem(i, 2) == 1, n // 2
    rising = lambda pair: (pair + 1) * parts // depth_z
    falling = lambda pair: (depth_z - 1 - pair) * parts // depth_z
    if n % 2 or n < 4:
        indirect = (0, 0)
        relayed = 0
    else:
        indirect = (jnp.where(odd, falling(z), 0), jnp.where(odd, 0, rising(z - 1)))
        relayed = jnp.where(odd, rising(z - 1), falling(z))
    via = (i - 1, i + 1)
    onward = jnp.where(odd, i - 2, i + 2)
    lands = (jnp.logical_not(odd), odd)
    relayed = jnp.where(odd, jnp.where(z > 0, relayed, 0), jnp.where(z < depth_z - 1, relayed, 0))
    loads = [
        pltpu.make_async_copy(src, dst, local_sem.at[t])
        for t, (src, dst) in enumerate(((f_hbm, f_ref), (o_hbm, o_ref), (k_hbm, k_ref), (r_hbm, r_ref)))
    ]
    for copy in loads:
        copy.start()
    core, along = ("gy", 1, 2), ("gx", 2, n // 2)
    ring = [(i, peer(index, core, 1)[2][1])]
    ring += [peer(index, along, k)[2] for k in range(1, n // 2)]
    corners = [(i, peer(index, ("gy", 2, 2), 1)[2][1]), (peer(index, ("gx", 1, 2), 1)[2][0], j)]
    corners.append((corners[1][0], corners[0][1]))
    greets = sides + ((i < n - 2, None, i + 2, j), (i > 1, None, i - 2, j))
    barrier = pltpu.get_barrier_semaphore()
    greeted = sum(has.astype(jnp.int32) for has, _, _, _ in greets)
    for has, _, a, b in greets:
        @pl.when(has)
        def _(a=a, b=b):
            pl.semaphore_signal(barrier, inc=1, device_id=(a, b), device_id_type=MESH)
    for device in ring + corners:
        pl.semaphore_signal(barrier, inc=1, device_id=device, device_id_type=MESH)
        greeted = greeted + 1
    with jax.named_scope("barrier"):
        pl.semaphore_wait(barrier, greeted)
    fields = (f_hbm, o_hbm, k_hbm)
    steps = blocks * parts

    def cut(at):
        c, q = divmod(at, parts)
        return pl.ds(q * step, step), pl.ds(c * LANES, LANES)

    def x_copies(side, at):
        _, _, a, b = sides[side]
        return [
            pltpu.make_async_remote_copy(
                src_ref=ref.at[((planes - 1, 0)[side],) + cut(at)],
                dst_ref=(xlo, xhi)[side].at[(t,) + cut(at)],
                send_sem=xs_sem.at[side],
                recv_sem=xr_sem.at[side, at],
                device_id=(a, b),
                device_id_type=MESH,
            )
            for t, ref in enumerate(fields)
        ]

    def to_relay(side, at):
        return [
            pltpu.make_async_remote_copy(
                src_ref=ref.at[((planes - 1, 0)[side],) + cut(at)],
                dst_ref=passing.at[(t,) + cut(at)],
                send_sem=xs_sem.at[side],
                recv_sem=pr_sem.at[at],
                device_id=(via[side], j),
                device_id_type=MESH,
            )
            for t, ref in enumerate(fields)
        ]

    def from_relay(side, at):
        return [
            pltpu.make_async_remote_copy(
                src_ref=passing.at[(t,) + cut(at)],
                dst_ref=(xlo, xhi)[side].at[(t,) + cut(at)],
                send_sem=ps_sem.at[0],
                recv_sem=xr_sem.at[side, at],
                device_id=(onward, j),
                device_id_type=MESH,
            )
            for t in range(3)
        ]

    def y_copies(side):
        _, _, a, b = sides[2 + side]
        return [
            pltpu.make_async_remote_copy(
                src_ref=ref.at[:, pl.ds((width - TILE, 0)[side], TILE)],
                dst_ref=(ylo, yhi)[side].at[t],
                send_sem=ys_sem.at[side],
                recv_sem=yr_sem.at[side],
                device_id=(a, b),
                device_id_type=MESH,
            )
            for t, ref in enumerate(fields)
        ]

    def whole(ref, send, recv, device=None):
        return pltpu.make_async_remote_copy(
            src_ref=ref, dst_ref=ref, send_sem=send, recv_sem=recv, device_id=device or (i, j), device_id_type=MESH
        )

    def post(at):
        for side in range(2):
            for lead in (LEAD, 0):
                late = at + lead
                if late >= steps:
                    continue

                @pl.when(sides[side][0] & ((late % parts < indirect[side]) if lead else (late % parts >= indirect[side])))
                def _(side=side, lead=lead, late=late):
                    for copy in (to_relay if lead else x_copies)(side, late):
                        copy.start()

    def forward(at):
        @pl.when(at % parts < relayed)
        def _():
            whole(passing.at[(slice(None),) + cut(at)], ps_sem.at[0], pr_sem.at[at]).wait_recv()

        for side in range(2):
            @pl.when((at % parts < relayed) & lands[side])
            def _(side=side):
                for copy in from_relay(side, at):
                    copy.start()

    row = lax.broadcasted_iota(jnp.int32, (step, LANES), 0)
    lane = lax.broadcasted_iota(jnp.int32, (step, LANES), 1)
    refs = (f_ref, o_ref, k_ref)
    zero = jnp.zeros((step, LANES), jnp.float32)
    zrow = jnp.zeros((1, LANES), jnp.float32)
    columns = (((0,), (0,)), ((), ()))
    products = (((1,), (0,)), ((), ()))

    def dot(left, right, dims):
        return lax.dot_general(left, right, dims, precision=HIGHEST, preferred_element_type=jnp.float32)

    def arrive(at):
        for late in range(0 if at == 0 else at + LEAD, min(at + LEAD + 1, steps)):
            forward(late)
        for side in range(2):
            @pl.when(sides[side][1])
            def _(side=side):
                whole((xlo, xhi)[side].at[(slice(None),) + cut(at)], xs_sem.at[side], xr_sem.at[side, at]).wait_recv()

    def advance(at):
        c, q = divmod(at, parts)
        y = q * step
        here = cut(at)
        cols = here[1]
        for x in range(planes):
            center = [ref[(x,) + here] for ref in refs]
            sets = []
            if x == 0:
                sets.append([jnp.where(i > 0, xlo[(t,) + here], zero) for t in range(3)])
            else:
                sets.append([ref[(x - 1,) + here] for ref in refs])
            if x == planes - 1:
                sets.append([jnp.where(i < n - 1, xhi[(t,) + here], zero) for t in range(3)])
            else:
                sets.append([ref[(x + 1,) + here] for ref in refs])
            if y == 0:
                before = [jnp.where(j > 0, ylo[t, x, TILE - 1:TILE, cols], zrow) for t in range(3)]
            else:
                before = [ref[x, y - 1:y, cols] for ref in refs]
            if y + step == width:
                after = [jnp.where(j < m - 1, yhi[t, x, 0:1, cols], zrow) for t in range(3)]
            else:
                after = [ref[x, y + step:y + step + 1, cols] for ref in refs]
            sets.append([jnp.where(row == 0, b, pltpu.roll(v, 1, 0)) for b, v in zip(before, center)])
            sets.append([jnp.where(row == step - 1, a, pltpu.roll(v, step - 1, 0)) for a, v in zip(after, center)])
            if c:
                left = [pltpu.roll(ref[x, here[0], pl.ds((c - 1) * LANES, LANES)], 1, 1) for ref in refs]
            else:
                left = [zero] * 3
            if c < blocks - 1:
                right = [pltpu.roll(ref[x, here[0], pl.ds((c + 1) * LANES, LANES)], LANES - 1, 1) for ref in refs]
            else:
                right = [zero] * 3
            sets.append([jnp.where(lane == 0, b, pltpu.roll(v, 1, 1)) for b, v in zip(left, center)])
            sets.append([jnp.where(lane == LANES - 1, a, pltpu.roll(v, LANES - 1, 1)) for a, v in zip(right, center)])
            fc, oc, kc = center
            df, do = zero, zero
            for fs, os, ks in sets:
                weight = 0.5 * (kc + ks)
                df = df + weight * (fs - fc)
                do = do + weight * (os - oc)
            prod = fc * oc
            react = r_ref[(x,) + here] * prod / jnp.sqrt(1.0 + prod * prod)
            fn_ref[(x,) + here] = fc + 0.15 * (df - react)
            on_ref[(x,) + here] = oc + 0.15 * (do + react)
        to = (c + 1) * LANES
        u = jnp.concatenate([ref[x, here[0], :to] for ref in (fn_ref, on_ref) for x in range(planes)], axis=0)
        total = dot(u, u[:, c * LANES:], columns)
        grams[c][...] = total if q == 0 else grams[c][...] + total

    def sends(c, s, source, target, devices):
        return [
            pltpu.make_async_remote_copy(
                src_ref=source(*to),
                dst_ref=target(*to),
                send_sem=as_sem.at[c, s],
                recv_sem=ar_sem.at[c, s],
                device_id=device,
                device_id_type=MESH,
            )
            for to, device in devices
        ]

    def span(at, length):
        return pl.ds(pl.multiple_of(at * length, TILE), length)

    half = [(c + 1) * LANES // 2 for c in range(blocks)]
    piece = [length // (n // 2) for length in half]
    mine_core, mine_along = lax.rem(j, 2), i // 2
    beside = [((1 - mine_core, 0), ring[0])]
    others = [((lax.rem(mine_along + k, n // 2), k - 1), ring[k]) for k in range(1, n // 2)]
    around = [((0, k), corners[k]) for k in range(3)]

    def whole_slot(c):
        start = mine_core * half[c] + mine_along * piece[c]
        return pl.ds(pl.multiple_of(start, TILE), piece[c])

    def exchange(c, s):
        if s == 0:
            return sends(c, 0, lambda a, k: grams[c].at[span(a, half[c])], lambda a, k: inbox[c], beside)
        if s == 1:
            return sends(c, 1, lambda a, k: held[c].at[span(a, piece[c])], lambda a, k: inbox_x[c].at[k], others)
        if s == 2:
            return sends(c, 2, lambda a, k: held_x[c], lambda a, k: inbox_z[c].at[k], around)
        if s == 3:
            slot = whole_slot(c)
            return sends(c, 3, lambda a, k: totals[c].at[slot], lambda a, k: totals[c].at[slot], others)
        part = span(mine_core, half[c])
        return sends(c, 4, lambda a, k: totals[c].at[part], lambda a, k: totals[c].at[part], beside)

    def landed(c, s):
        region = (inbox[c], inbox_x[c], inbox_z[c], inbox_x[c], inbox[c])[s]
        return whole(region, as_sem.at[c, s], ar_sem.at[c, s])

    def reduce_step(c, s):
        if s:
            landed(c, s - 1).wait_recv()
        if s == 1:
            held[c][...] = grams[c][span(mine_core, half[c])] + inbox[c][...]
        if s == 2:
            total = held[c][span(mine_along, piece[c])]
            for k in range(n // 2 - 1):
                total = total + inbox_x[c][k]
            held_x[c][...] = total
        if s == 3:
            total = (held_x[c][...] + inbox_z[c][0]) + (inbox_z[c][1] + inbox_z[c][2])
            totals[c][whole_slot(c)] = total / rows
        if s < 5:
            for copy in exchange(c, s):
                copy.start()

    eye = jnp.where(
        lax.broadcasted_iota(jnp.int32, (LANES, LANES), 0) == lax.broadcasted_iota(jnp.int32, (LANES, LANES), 1), 1.0, 0.0
    )

    def prepare(b):
        c0 = b * LANES
        panel, total = panels[b], totals[b]
        s = total[c0:c0 + LANES]
        if b:
            above = dot(w_out[:c0, :c0], total[:c0], products)
            rp_out[:c0, c0:c0 + LANES] = above
            s = s - dot(above, above, columns)
            panel[:, LANES:c0 + LANES] = -dot(above, w_out[:c0, :c0], columns)
        panel[:, :LANES] = s
        panel[:, c0 + LANES:] = eye
        if c0:
            rp_out[c0:c0 + LANES, :c0] = jnp.zeros((LANES, c0), jnp.float32)
        rest = w_out.shape[1] - c0 - LANES
        if rest:
            w_out[c0:c0 + LANES, c0 + LANES:] = jnp.zeros((LANES, rest), jnp.float32)

    def pivot(b, g):
        c0 = b * LANES

        def emit(q, t, strip):
            at = slice(c0 + q, c0 + q + TILE)
            if t == 0:
                rp_out[at, c0:c0 + LANES] = strip
            else:
                w_out[at, (t - 1) * LANES:t * LANES] = strip

        eliminate(panels[b], GROUP, g * GROUP * TILE, emit)

    groups = LANES // (TILE * GROUP)
    R = lambda c, s: functools.partial(reduce_step, c, s)
    prep = lambda b: functools.partial(prepare, b)
    C = lambda b, g: functools.partial(pivot, b, g)
    plan = {}
    if blocks == 3 and parts == 4 and groups == 4:
        plan = {
            3: [R(0, 0)], 4: [R(0, 1)], 6: [R(0, 2)], 7: [R(1, 0)], 8: [R(1, 1)], 9: [R(0, 3)],
            11: [
                R(2, 0), R(1, 2), R(2, 1), R(0, 4), R(0, 5), prep(0), C(0, 0), R(1, 3), C(0, 1), C(0, 2), R(2, 2), C(0, 3),
                R(1, 4), R(1, 5), prep(1), R(2, 3), C(1, 0), C(1, 1), C(1, 2), R(2, 4), C(1, 3), R(2, 5),
            ],
        }
    else:
        last = []
        for c in range(blocks):
            last += [R(c, s) for s in range(6)]
            if c < blocks - 1:
                last += [prep(c)] + [C(c, g) for g in range(groups)]
        plan = {steps - 1: last}
    for side in range(2):
        @pl.when(sides[2 + side][0])
        def _(side=side):
            for copy in y_copies(side):
                copy.start()
    for at in range(LEAD):
        for side in range(2):
            @pl.when(sides[side][0] & (at % parts < indirect[side]))
            def _(side=side, at=at):
                for copy in to_relay(side, at):
                    copy.start()
    for at in range(min(AHEAD, steps)):
        post(at)
    stores = [
        pltpu.make_async_copy(src, dst, local_sem.at[t])
        for t, (src, dst) in enumerate(((fn_ref, fn_hbm), (on_ref, on_hbm)))
    ]
    for at in range(steps):
        with jax.named_scope(f"w{at}"):
            arrive(at)
        if at + AHEAD < steps:
            post(at + AHEAD)
        if at == 0:
            for copy in loads:
                copy.wait()
            for side in range(2):
                @pl.when(sides[2 + side][1])
                def _(side=side):
                    whole((ylo, yhi)[side], ys_sem.at[side], yr_sem.at[side]).wait_recv()
        with jax.named_scope(f"s{at}"):
            advance(at)
        for task in plan.get(at, []):
            name = {"reduce_step": "R", "prepare": "P", "pivot": "C"}[task.func.__name__]
            with jax.named_scope(name + "".join(map(str, task.args))):
                task()
            if at == steps - 1 and task is plan[at][0]:
                for copy in stores:
                    copy.start()
    with jax.named_scope("sends"):
        for c in range(blocks):
            for s in range(5):
                landed(c, s).wait_send()
        for side in range(2):
            @pl.when(sides[2 + side][0])
            def _(side=side):
                whole((ylo, yhi)[side], ys_sem.at[side], yr_sem.at[side]).wait_send()

            @pl.when(sides[side][0])
            def _(side=side):
                whole((xlo, xhi)[side], xs_sem.at[side], xr_sem.at[side, 0]).wait_send()

        for count in range(1, parts):
            @pl.when(relayed == count)
            def _(count=count):
                whole(passing.at[:, pl.ds(0, count * step)], ps_sem.at[0], pr_sem.at[0]).wait_send()
        for copy in stores:
            copy.wait()


def early(n, m, rows, fuel, oxidizer, kappa, rate):
    planes, width, depth = fuel.shape
    blocks = depth // LANES
    parts = 4 if width % (4 * TILE) == 0 else 1
    steps = blocks * parts
    size = [(c + 1) * LANES for c in range(blocks)]
    vmem = lambda *shape: pltpu.VMEM(shape, jnp.float32)
    inner = depth - LANES
    scratch = [vmem(*fuel.shape)] * 6
    scratch += [vmem(3, width, depth)] * 2
    scratch += [vmem(3, planes, TILE, depth)] * 2
    scratch += [vmem(3, width, depth)]
    scratch += [pltpu.SemaphoreType.DMA((4,))]
    scratch += [pltpu.SemaphoreType.DMA((2,)), pltpu.SemaphoreType.DMA((2, steps))]
    scratch += [pltpu.SemaphoreType.DMA((2,))] * 2
    scratch += [pltpu.SemaphoreType.DMA((1,)), pltpu.SemaphoreType.DMA((steps,))]
    scratch += [pltpu.SemaphoreType.DMA((blocks, 5))] * 2
    scratch += [vmem(length, LANES) for length in size]
    scratch += [vmem(length // 2, LANES) for length in size] * 2
    scratch += [vmem(n // 2 - 1, length // n, LANES) for length in size]
    scratch += [vmem(length // n, LANES) for length in size]
    scratch += [vmem(3, length // n, LANES) for length in size]
    scratch += [vmem(length, LANES) for length in size[:-1]]
    scratch += [vmem(LANES, (b + 2) * LANES) for b in range(blocks - 1)]
    field = jax.ShapeDtypeStruct(fuel.shape, jnp.float32)
    any_spec = pl.BlockSpec(memory_space=pl.ANY)
    vmem_spec = pl.BlockSpec(memory_space=pltpu.VMEM)
    return pl.pallas_call(
        functools.partial(early_kernel, n, m, rows, parts),
        out_shape=(field, field, vmem(depth, LANES), vmem(inner, inner), vmem(inner, inner)),
        in_specs=[any_spec] * 4,
        out_specs=(any_spec, any_spec, vmem_spec, vmem_spec, vmem_spec),
        scratch_shapes=scratch,
        compiler_params=pltpu.CompilerParams(collective_id=0, has_side_effects=True),
        name="early",
    )(fuel, oxidizer, kappa, rate)


def finish_kernel(g_ref, w_ref, rp_ref, fn_in, on_in, r_out, fn_out, on_out, a_ref, r_ref, fn_ref, on_ref, sems, r_sems):
    loads = [pltpu.make_async_copy(fn_in, fn_ref, sems.at[0]), pltpu.make_async_copy(on_in, on_ref, sems.at[1])]
    stores = [pltpu.make_async_copy(fn_ref, fn_out, sems.at[2]), pltpu.make_async_copy(on_ref, on_out, sems.at[3])]
    for copy in loads:
        copy.start()
    inner = w_ref.shape[0]
    tall = GROUP * TILE
    dot = functools.partial(lax.dot_general, precision=HIGHEST, preferred_element_type=jnp.float32)
    above = dot(w_ref[...], g_ref[:inner], (((1,), (0,)), ((), ())))
    a_ref[...] = g_ref[inner:] - dot(above, above, (((0,), (0,)), ((), ())))
    r_ref[:inner, :inner] = rp_ref[...]
    r_ref[:inner, inner:] = above
    r_ref[inner:, :inner] = jnp.zeros((LANES, inner), jnp.float32)

    def emit(q, t, strip):
        r_ref[inner + q:inner + q + TILE, inner:] = strip

    def write(first, length, at):
        return pltpu.make_async_copy(r_ref.at[pl.ds(first, length)], r_out.at[pl.ds(first, length)], r_sems.at[at])

    writes = [write(0, inner, 0)]
    for first in range(0, LANES, tall):
        eliminate(a_ref, GROUP, first, emit)
        writes.append(write(inner + first, tall, 1 + first // tall))
        for copy in writes[-2 if first == 0 else -1:]:
            copy.start()
        if first == 0:
            for load, store in zip(loads, stores):
                load.wait()
                store.start()
    for copy in writes + stores:
        copy.wait()


def finish(gram, inverse, upper, fuel_next, oxid_next):
    depth = fuel_next.shape[2]
    field = jax.ShapeDtypeStruct(fuel_next.shape, jnp.float32)
    vmem = pl.BlockSpec(memory_space=pltpu.VMEM)
    any_spec = pl.BlockSpec(memory_space=pl.ANY)
    gram, inverse, upper = (pltpu.with_memory_space_constraint(v, pltpu.VMEM) for v in (gram, inverse, upper))
    return pl.pallas_call(
        finish_kernel,
        out_shape=(jax.ShapeDtypeStruct((depth, depth), jnp.float32), field, field),
        in_specs=[vmem, vmem, vmem, any_spec, any_spec],
        out_specs=(any_spec, any_spec, any_spec),
        scratch_shapes=[
            pltpu.VMEM((LANES, LANES), jnp.float32),
            pltpu.VMEM((depth, depth), jnp.float32),
            pltpu.VMEM(fuel_next.shape, jnp.float32),
            pltpu.VMEM(fuel_next.shape, jnp.float32),
            pltpu.SemaphoreType.DMA((4,)),
            pltpu.SemaphoreType.DMA((1 + LANES // (GROUP * TILE),)),
        ],
        name="finish",
        compiler_params=pltpu.CompilerParams(),
    )(gram, inverse, upper, fuel_next, oxid_next)


def stacked_dot(left, right):
    dims = (((0,), (0,)), ((), ()))
    def pieces(v):
        h = v.astype(jnp.bfloat16).astype(jnp.float32)
        m = (v - h).astype(jnp.bfloat16).astype(jnp.float32)
        return h, m, v - h - m
    (a, b, c), (d, e, f) = pieces(left), pieces(right)
    lhs = jnp.concatenate([a, a, b, a, c, b], axis=0).astype(jnp.bfloat16)
    rhs = jnp.concatenate([d, e, d, f, d, e], axis=0).astype(jnp.bfloat16)
    return lax.dot_general(lhs, rhs, dims, preferred_element_type=jnp.float32)


def column_of(panel, at):
    return jnp.broadcast_to(panel[:, at:at + 1], (TILE, LANES))


def factor_kernel(group, g_ref, fn_in, on_in, r_ref, fn_out, on_out, a_ref, fn_ref, on_ref, sems):
    loads = [pltpu.make_async_copy(fn_in, fn_ref, sems.at[0]), pltpu.make_async_copy(on_in, on_ref, sems.at[1])]
    stores = [pltpu.make_async_copy(fn_ref, fn_out, sems.at[2]), pltpu.make_async_copy(on_ref, on_out, sems.at[3])]
    for copy in loads:
        copy.start()
    depth = r_ref.shape[0]
    blocks = depth // LANES
    at = 0
    for b in range(blocks):
        for c in range(b, blocks):
            a_ref[b * LANES:(b + 1) * LANES, c * LANES:(c + 1) * LANES] = g_ref[at:at + LANES]
            at += LANES
    dims = (((0,), (0,)), ((), ()))
    dot = functools.partial(lax.dot_general, dimension_numbers=dims, precision=HIGHEST, preferred_element_type=jnp.float32)
    sub = lax.broadcasted_iota(jnp.int32, (TILE, LANES), 0)
    lane = lax.broadcasted_iota(jnp.int32, (TILE, LANES), 1)
    for b in range(blocks):
        c0 = b * LANES
        tiles = range(blocks - b)
        if c0:
            r_ref[c0:c0 + LANES, :c0] = jnp.zeros((LANES, c0), jnp.float32)
        for p in range(0, LANES, TILE * group):
            before = []
            for q in range(p, p + TILE * group, TILE):
                r0 = c0 + q
                strips = [a_ref[r0:r0 + TILE, c0 + t * LANES:c0 + (t + 1) * LANES] for t in tiles]
                for s, inv, low, rows in before:
                    factors = []
                    for k in range(TILE):
                        value = column_of(strips[0], s + k)
                        for j in range(k):
                            value = value - factors[j] * low[k, j]
                        factors.append(value * inv[k])
                    for t in tiles:
                        for k in range(TILE):
                            strips[t] = strips[t] - factors[k] * rows[t][k]
                e = {}
                for k in range(TILE):
                    column = column_of(strips[0], q + k)
                    for i in range(k, TILE):
                        e[i, k] = jnp.broadcast_to(column[i:i + 1], (TILE, LANES))
                inv, low = [], {}
                for k in range(TILE):
                    inv.append(lax.rsqrt(e[k, k]))
                    for i in range(k + 1, TILE):
                        low[i, k] = e[i, k] * inv[k]
                    for j in range(k + 1, TILE):
                        for i in range(j, TILE):
                            e[i, j] = e[i, j] - low[i, k] * low[j, k]
                rows = []
                for t in tiles:
                    made = []
                    for k in range(TILE):
                        value = jnp.broadcast_to(strips[t][k:k + 1], (TILE, LANES))
                        for j in range(k):
                            value = value - low[k, j] * made[j]
                        made.append(value * inv[k])
                    rows.append(made)
                    strip = made[0]
                    for k in range(1, TILE):
                        strip = jnp.where(sub == k, made[k], strip)
                    if t == 0:
                        strip = jnp.where(lane >= sub + q, strip, 0.0)
                    r_ref[r0:r0 + TILE, c0 + t * LANES:c0 + (t + 1) * LANES] = strip
                before.append((q, inv, low, rows))
            low_end = p + TILE * group
            if low_end < LANES:
                upper = r_ref[c0 + p:c0 + low_end, c0:]
                a_ref[c0 + low_end:c0 + LANES, c0:] -= stacked_dot(upper[:, :LANES], upper)[low_end:]
        if b == 0:
            for load, store in zip(loads, stores):
                load.wait()
                store.start()
        for d in range(b + 1, blocks):
            d0 = d * LANES
            a_ref[d0:d0 + LANES, d0:] -= dot(r_ref[c0:c0 + LANES, d0:d0 + LANES], r_ref[c0:c0 + LANES, d0:])
    for copy in stores:
        copy.wait()


def factor(gram, fuel_next, oxid_next):
    depth = fuel_next.shape[2]
    field = jax.ShapeDtypeStruct(fuel_next.shape, jnp.float32)
    vmem = pl.BlockSpec(memory_space=pltpu.VMEM)
    any_spec = pl.BlockSpec(memory_space=pl.ANY)
    return pl.pallas_call(
        functools.partial(factor_kernel, 4),
        out_shape=(jax.ShapeDtypeStruct((depth, depth), jnp.float32), field, field),
        in_specs=[vmem, any_spec, any_spec],
        out_specs=(vmem, any_spec, any_spec),
        scratch_shapes=[
            pltpu.VMEM((depth, depth), jnp.float32),
            pltpu.VMEM(fuel_next.shape, jnp.float32),
            pltpu.VMEM(fuel_next.shape, jnp.float32),
            pltpu.SemaphoreType.DMA((4,)),
        ],
        name="factor",
    )(gram, fuel_next, oxid_next)


def shards(n, m, fuel, oxidizer, kappa, rate):
    planes, width, depth = fuel.shape
    rows = 2 * planes * width * n * m
    blocks = depth // LANES
    if blocks > 1 and m == 4 and n % 2 == 0 and n >= 4 and LANES % (TILE * n) == 0:
        fuel_next, oxid_next, gram, inverse, upper = early(n, m, rows, fuel, oxidizer, kappa, rate)
        r_factor, fuel_next, oxid_next = finish(gram, inverse, upper, fuel_next, oxid_next)
        return (fuel_next, oxid_next, r_factor)
    fuel_next, oxid_next, gram = update(n, m, rows, (), fuel, oxidizer, kappa, rate)
    gram = lax.psum(gram, ("gx", "gy"))
    r_factor, fuel_next, oxid_next = factor(gram, fuel_next, oxid_next)
    return (fuel_next, oxid_next, r_factor)


def solution(mesh):
    spec = P("gx", "gy", None)
    body = functools.partial(shards, mesh.shape["gx"], mesh.shape["gy"])
    return jax.shard_map(body, mesh=mesh, in_specs=(spec,) * 4, out_specs=(spec, spec, P()), check_vma=False)
```
